128 devices in a mesh: tm: 16 (over z, y_hi, core), space: 8 (over y_lo, x).
Axes of the slice: x: 4, y: 4 (y_hi: 2, y_lo: 2; y = y_hi * 2 + y_lo), z: 4, core: 2. Of those that a mesh axis runs over, the one named last changes fastest.
Arguments:
- start_states: float32 [16, 2, 12, 384, 256], P('tm', None, None, 'space'), may hold values from -6 to 6
- wet_levels: int32 [384, 256], P('space'), may hold values from 0 to 12
- advection: float32 [384, 256], P('space'), may hold values from 0.05 to 0.3
- forcing: float32 [384, 256], P('space'), may hold values from -6 to 6
- rates: float32 [4, 12], replicated, may hold values from 0.02 to 0.12
Outputs:
- new_states: float32 [16, 2, 12, 384, 256], P('tm', None, None, 'space')
The draws below stay inside these ranges and needn't reach their ends.
All inputs are finite; a program needn't handle non-finite values.
Results may differ from the reference program's by a relative error of at most 0.00002.
Values sent between devices are 32-bit elements; how exact they have to be, the bound alone decides.
No kernel may reach another device: no remote copies, remote signals or barrier semaphores. Data moves between devices by JAX's collectives and lax.ppermute only.
A program may use at most 128 MiB of HBM per device.

```python
import math
import jax
import jax.numpy as jnp
from jax import lax

TR = 2
LEV = 12
LAT = 256
STEPS = 4
SECTIONS = 4
COARSEN = 4
SEG = 16
NLON = 384
N_TM = 16


def plant(result, stream_key, smallest, top_value):
    spot = [jax.random.randint(jax.random.fold_in(stream_key, axis), (), 0, length) for axis, length in enumerate(result.shape)]
    main_axis = result.shape.index(max(result.shape))
    neighbour = spot[:main_axis] + [(spot[main_axis] + 1) % result.shape[main_axis]] + spot[main_axis + 1:]
    return result.at[tuple(spot)].set(smallest).at[tuple(neighbour)].set(top_value)


def block_scale(own_key, extent, cuts, least, top_value):
    gain, own = 1.0, jax.random.fold_in(own_key, 6)
    for dim, shards_of in cuts:
        steps = jnp.exp(jax.random.uniform(jax.random.fold_in(own, dim), (shards_of,), jnp.float32, least / len(cuts), top_value / len(cuts)))
        gain = gain * jnp.repeat(steps, extent[dim] // shards_of).reshape([-1 if axis == dim else 1 for axis in range(len(extent))])
    return gain


def normal_values(key, shape, scale, reach, cuts=(), kind=jnp.bfloat16):
    entries = scale * jax.random.normal(key, shape, jnp.float32)
    if cuts:
        entries = entries * block_scale(key, shape, cuts, -0.22, 0.18)
    return jnp.clip(entries, -reach, reach).astype(kind)


def setup_inputs(seed: int = 0) -> dict:
    splits = jax.random.split(jax.random.key(seed), 6)
    return {
        "start_states": normal_values(splits[0], (SEG, TR, LEV, NLON, LAT), 1.0, 6.0, ((0, 16), (3, 8)), jnp.float32),
        "wet_levels": plant(jax.random.randint(splits[1], (NLON, LAT), 0, LEV + 1), jax.random.fold_in(splits[1], 1), 0, LEV).astype(jnp.int32),
        "advection": jnp.clip(0.05 + 0.25 * jax.random.uniform(splits[2], (NLON, LAT), jnp.float32) ** block_scale(splits[2], (NLON, LAT), ((0, 8),), -0.2, 0.2), 0.05, 0.3),
        "forcing": normal_values(splits[3], (NLON, LAT), 1.0, 6.0, ((0, 8),), jnp.float32),
        "rates": jnp.clip(jnp.exp(jax.random.uniform(splits[4], (4, LEV), jnp.float32, math.log(0.02), math.log(0.12))), 0.02, 0.12),
    }


def pad_lon(field, width):
    return jnp.concatenate([field[..., -width:, :], field, field[..., :width, :]], axis=-2)


def restrict(field):
    shape = field.shape[:-2] + (field.shape[-2] // COARSEN, COARSEN, field.shape[-1] // COARSEN, COARSEN)
    return jnp.mean(field.reshape(shape), axis=(-3, -1))


def prolong(field):
    return jnp.repeat(jnp.repeat(field, COARSEN, axis=-2), COARSEN, axis=-1)


def season_at(position, year):
    return 1.0 + 0.6 * jnp.sin(2.0 * math.pi * position / year)


def advance(padded, mask_pad, flow_rate, forcing, coeffs, relax, season):
    kappa, vertical, growth, remin = coeffs[0], coeffs[1], coeffs[2], coeffs[3]
    centre = padded[:, :, 1:-1, :]
    mask = mask_pad[:, 1:-1, :]
    east = padded[:, :, 2:, :]
    west = padded[:, :, :-2, :]
    mask_east = mask_pad[:, 2:, :]
    mask_west = mask_pad[:, :-2, :]
    zero_row = jnp.zeros(centre.shape[:-1] + (1,), jnp.float32)
    north = jnp.concatenate([centre[..., 1:], zero_row], axis=-1)
    south = jnp.concatenate([zero_row, centre[..., :-1]], axis=-1)
    zero_mrow = jnp.zeros(mask.shape[:-1] + (1,), jnp.float32)
    mask_north = jnp.concatenate([mask[..., 1:], zero_mrow], axis=-1)
    mask_south = jnp.concatenate([zero_mrow, mask[..., :-1]], axis=-1)
    spread = (mask_east * (east - centre) + mask_west * (west - centre)
              + mask_north * (north - centre) + mask_south * (south - centre))
    carried = flow_rate * mask_west * (west - centre)
    zero_level = jnp.zeros((centre.shape[0], 1) + centre.shape[2:], jnp.float32)
    deeper = jnp.concatenate([centre[:, 1:], zero_level], axis=1)
    shallower = jnp.concatenate([zero_level, centre[:, :-1]], axis=1)
    zero_layer = jnp.zeros((1,) + mask.shape[1:], jnp.float32)
    mask_deeper = jnp.concatenate([mask[1:], zero_layer], axis=0)
    mask_shallower = jnp.concatenate([zero_layer, mask[:-1]], axis=0)
    upper_rate = jnp.concatenate([jnp.zeros((1,), jnp.float32), vertical[:-1]])
    column = (vertical[:, None, None] * mask_deeper * (deeper - centre)
              + upper_rate[:, None, None] * mask_shallower * (shallower - centre))
    mixed = centre + kappa[:, None, None] * spread + carried + column
    produced = growth[:, None, None] * season * mixed[0]
    respired = remin[:, None, None] * mixed[1]
    nutrient = mixed[0] - produced + respired
    nutrient = nutrient.at[0].add(relax * (forcing - mixed[0, 0]))
    organic = mixed[1] + produced - respired
    return mask * jnp.stack([nutrient, organic])


def reference(start_states, wet_levels, advection, forcing, rates):
    levels = jnp.arange(LEV).astype(jnp.int32)
    mask = (levels[:, None, None] < wet_levels[None]).astype(jnp.float32)
    mask_pad = pad_lon(mask, 1)
    coarse_mask_pad = pad_lon(restrict(mask), 1)
    coarse_flow = restrict(advection) * (STEPS / COARSEN)
    coarse_forcing = restrict(forcing)
    scale = jnp.array([STEPS / COARSEN ** 2, STEPS, STEPS, STEPS], jnp.float32)
    coarse_rates = rates * scale[:, None]
    year = STEPS * N_TM
    segments = jnp.arange(N_TM).astype(jnp.float32)

    def fine_segment(inputs):
        state, seg = inputs
        for step in range(STEPS):
            state = advance(pad_lon(state, 1), mask_pad, advection, forcing, rates, 0.2,
                            season_at(seg * STEPS + step + 0.5, year))
        return state

    def coarse_one(coarse, seg):
        return advance(pad_lon(coarse, 1), coarse_mask_pad, coarse_flow, coarse_forcing, coarse_rates,
                       0.2 * STEPS, season_at(seg * STEPS + STEPS * 0.5, year))

    def coarse_all(coarse):
        return jax.vmap(coarse_one)(coarse, segments)

    fine_end = lax.map(fine_segment, (start_states, segments))
    restricted = restrict(start_states)
    jump = fine_end - prolong(coarse_all(restricted))
    jump_coarse = restrict(jump)
    coarse = restricted
    for section in range(SECTIONS):
        coarse = jnp.roll(coarse_all(coarse) + jump_coarse, 1, axis=0)
    return jnp.roll(prolong(coarse_all(coarse)) + jump, 1, axis=0)
```

```python
import functools
import math

import jax
import jax.numpy as jnp
from jax import lax
from jax.experimental import pallas as pl
from jax.experimental.pallas import tpu as pltpu
from jax.sharding import PartitionSpec as P

STEPS = 4
SECTIONS = 4
COARSEN = 4
RELAX = 0.2
LANES = 128
ROWS = 16
F32 = jnp.float32
HIGH = lax.Precision.HIGHEST


def season_of(segment, count, offset):
    year = STEPS * count
    value = jnp.float32(0.0)
    for i in range(count):
        here = 1.0 + 0.6 * math.sin(2.0 * math.pi * (i * STEPS + offset) / year)
        value = jnp.where(segment == i, jnp.float32(here), value)
    return value


def iota(shape, axis):
    return lax.broadcasted_iota(jnp.int32, shape, axis)


def mean_matrix(tracer):
    shape = (2 * LANES, LANES)
    target = lax.shift_right_logical(iota(shape, 0), 2)
    lane = iota(shape, 1)
    weight = jnp.float32(1.0 / COARSEN**2)
    if tracer is None:
        return jnp.where((lane & 63) == target, weight, 0.0)
    return jnp.where(lane == target + 64 * tracer, weight, 0.0)


def spread_matrix(tracer):
    shape = (LANES, 2 * LANES)
    source = lax.shift_right_logical(iota(shape, 1), 2) + 64 * tracer
    return jnp.where(iota(shape, 0) == source, 1.0, 0.0).astype(F32)


def planes_of(rates, levels):
    shape = (ROWS, LANES)
    level, lane = iota(shape, 0), iota(shape, 1)
    zero = jnp.zeros(shape, F32)
    k, below, above, grow, remin = zero, zero, zero, zero, zero
    for l in range(levels):
        here = level == l
        k = jnp.where(here, rates[0, l] * (STEPS / COARSEN**2), k)
        if l < levels - 1:
            below = jnp.where(here, rates[1, l] * STEPS, below)
        if l > 0:
            above = jnp.where(here, rates[1, l - 1] * STEPS, above)
        grow = jnp.where(here, rates[2, l] * STEPS, grow)
        remin = jnp.where(here, rates[3, l] * STEPS, remin)
    return {
        "k": k,
        "kn": jnp.where((lane & 63) != 63, k, 0.0),
        "ks": jnp.where((lane & 63) != 0, k, 0.0),
        "below": below,
        "above": above,
        "grow": grow,
        "remin": remin,
        "first": lane < 64,
        "side": jnp.where(lane < 64, -1.0, 1.0).astype(F32),
        "relax": jnp.where((lane < 64) & (level == 0), RELAX * STEPS, 0.0).astype(F32),
    }


def turned(block, shift, axis):
    flat = block.reshape(block.shape[0] * ROWS, LANES)
    return pltpu.roll(flat, shift % flat.shape[axis], axis).reshape(block.shape)


def coarse_weights(mask, flow, p):
    inner = mask[1:-1]
    return (
        1.0
        - p["k"] * (mask[2:] + mask[:-2])
        - p["kn"] * turned(inner, -1, 1)
        - p["ks"] * turned(inner, 1, 1)
        - flow * mask[:-2]
        - p["below"] * turned(inner, -1, 0)
        - p["above"] * turned(inner, 1, 0)
    )


def coarse_step(coarse, mask, weight, flow, relaxed, season, p):
    wet = coarse * mask
    inner = wet[1:-1]
    mixed = (
        weight * coarse[1:-1]
        + p["k"] * (wet[2:] + wet[:-2])
        + p["kn"] * turned(inner, -1, 1)
        + p["ks"] * turned(inner, 1, 1)
        + flow * wet[:-2]
        + p["below"] * turned(inner, -1, 0)
        + p["above"] * turned(inner, 1, 0)
    )
    part = mixed * jnp.where(p["first"], p["grow"] * season, -p["remin"])
    change = part + turned(part, 64, 1)
    return mask[1:-1] * (mixed + p["side"] * change - p["relax"] * mixed + relaxed)


def fine_kernel(
    count, x, hl, hr, wet, adv, forc, rates,
    fine_out, rf_out, rj_out, stat_out,
    u, c0, mk, wets, flow, force, sums, table, cols,
):
    levels = x.shape[1]
    own = x.shape[2]
    total = own + 2 * COARSEN
    ncol = total // COARSEN
    segment = lax.axis_index("tm")
    halves = [slice(0, LANES), slice(LANES, 2 * LANES)]
    lane = iota((total, LANES), 1)
    first, last = lane == 0, lane == LANES - 1
    tracers = x.shape[0]

    def lay(dst, plane, halo_plane, h):
        dst[0:own, :] = plane[:, halves[h]].astype(F32)
        dst[own : own + COARSEN, :] = hr[halo_plane, :, halves[h]]
        dst[own + COARSEN : total, :] = hl[halo_plane, :, halves[h]]

    base = tracers * levels
    for h in range(2):
        lay(wets.at[0, h], wet, base, h)
        lay(flow.at[h], adv, base + 1, h)
        lay(force.at[h], forc, base + 2, h)
        for t in range(tracers):
            for l in range(levels):
                lay(u.at[1, t, l + 1, h], x.at[t, l], t * levels + l, h)
    for b in range(2):
        for t in range(tracers):
            for edge in (0, levels + 1):
                for h in range(2):
                    u[b, t, edge, h] = jnp.zeros((total, LANES), F32)

    def north_south(plane):
        ahead = [pltpu.roll(plane[h], LANES - 1, 1) for h in range(2)]
        behind = [pltpu.roll(plane[h], 1, 1) for h in range(2)]
        north = [jnp.where(last, ahead[1], ahead[0]), jnp.where(last, 0.0, ahead[1])]
        south = [jnp.where(first, 0.0, behind[0]), jnp.where(first, behind[0], behind[1])]
        return north, south

    plane = [wets[0, h] for h in range(2)]
    north, south = north_south(plane)
    for h in range(2):
        wets[1, h] = pltpu.roll(plane[h], total - 1, 0)
        wets[2, h] = pltpu.roll(plane[h], 1, 0)
        wets[3, h] = north[h]
        wets[4, h] = south[h]

    def weights(l, _):
        depth = l.astype(F32)
        k = rates[0, l]
        below = rates[1, l]
        above = jnp.where(l > 0, rates[1, jnp.maximum(l - 1, 0)], 0.0)
        for h in range(2):
            own_wet = wets[0, h]
            value = jnp.full((total, LANES), 1.0 - above, F32)
            value = value - jnp.where(own_wet > depth + 1.0, below, 0.0)
            value = value - jnp.where(wets[1, h] > depth, k, 0.0)
            value = value - jnp.where(wets[3, h] > depth, k, 0.0)
            value = value - jnp.where(wets[4, h] > depth, k, 0.0)
            value = value - jnp.where(wets[2, h] > depth, k + flow[h], 0.0)
            c0[l, h] = value
            inside = own_wet > depth
            mk[l, h] = jnp.where(inside, 1.0, 0.0)
            for t in range(tracers):
                u[0, t, l + 1, h] = jnp.where(inside, u[1, t, l + 1, h], 0.0)
        return 0

    def block_sum(ref):
        value = ref[pl.ds(0, ncol, stride=COARSEN), :]
        for k in range(1, COARSEN):
            value = value + ref[pl.ds(k, ncol, stride=COARSEN), :]
        return value

    def restrict(b, dst):
        def gather(l, _):
            at = pl.multiple_of(l * ROWS, ROWS)
            for t in range(tracers):
                for h in range(2):
                    sums[t, pl.ds(at, ncol), halves[h]] = block_sum(u.at[b, t, l + 1, h])
            return 0

        lax.fori_loop(0, levels, gather, 0)
        value = jnp.dot(sums[0], mean_matrix(0), precision=HIGH, preferred_element_type=F32)
        value += jnp.dot(sums[1], mean_matrix(1), precision=HIGH, preferred_element_type=F32)
        table[...] = value
        for c in range(ncol):
            dst[c, 0:levels, :] = table[pl.ds(c, levels, stride=ROWS), :]
            dst[c, levels:ROWS, :] = jnp.zeros((ROWS - levels, LANES), F32)

    sums[...] = jnp.zeros(sums.shape, F32)
    restrict(1, cols.at[0])
    lax.fori_loop(0, levels, weights, 0)

    def gather_static(l, _):
        at = pl.multiple_of(l * ROWS, ROWS)
        for h in range(2):
            sums[0, pl.ds(at, ncol), halves[h]] = block_sum(mk.at[l, h])
        return 0

    lax.fori_loop(0, levels, gather_static, 0)
    for h in range(2):
        sums[0, pl.ds(levels * ROWS, ncol), halves[h]] = block_sum(flow.at[h])
        sums[0, pl.ds((levels + 1) * ROWS, ncol), halves[h]] = block_sum(force.at[h])
    wide = jnp.dot(
        sums[0, 0 : (levels + 2) * ROWS], mean_matrix(None),
        precision=HIGH, preferred_element_type=F32,
    )
    table[0 : (levels + 2) * ROWS, :] = wide
    for c in range(ncol):
        cols[1, c, 0 : levels + 2, :] = table[pl.ds(c, levels + 2, stride=ROWS), :]
        cols[1, c, levels + 2 : ROWS, :] = jnp.zeros((ROWS - levels - 2, LANES), F32)

    for step in range(STEPS):
        old, new = step % 2, (step + 1) % 2
        season = season_of(segment, count, step + 0.5)

        def level(l, relax, old=old, new=new, season=season):
            k = rates[0, l]
            below = rates[1, l]
            above = rates[1, jnp.maximum(l - 1, 0)]
            grow, remin = rates[2, l] * season, rates[3, l]
            mixed = []
            for t in range(tracers):
                here = [u[old, t, l + 1, h] for h in range(2)]
                north, south = north_south(here)
                row = []
                for h in range(2):
                    east = pltpu.roll(here[h], total - 1, 0)
                    west = pltpu.roll(here[h], 1, 0)
                    row.append(
                        c0[l, h] * here[h]
                        + k * (east + north[h] + south[h])
                        + (flow[h] + k) * west
                        + below * u[old, t, l + 2, h]
                        + above * u[old, t, l, h]
                    )
                mixed.append(row)
            for h in range(2):
                w0, w1 = mixed[0][h], mixed[1][h]
                change = grow * w0 - remin * w1
                nutrient = w0 - change
                if relax:
                    nutrient = nutrient + RELAX * (force[h] - w0)
                inside = mk[l, h]
                u[new, 0, l + 1, h] = inside * nutrient
                u[new, 1, l + 1, h] = inside * (w1 + change)

        level(0, True)

        def rest(l, _, level=level):
            level(l, False)
            return 0

        lax.fori_loop(1, levels, rest, 0)

    end = STEPS % 2
    restrict(end, cols.at[2])

    p = planes_of(rates, levels)
    order = [ncol - 1] + list(range(ncol - 1))
    row = iota((ROWS, LANES), 0)

    def natural(which):
        return jnp.stack([cols[which, c] for c in order])

    def spread_row(which, r):
        return jnp.stack([cols[which, c, pl.ds(r, ROWS, stride=0), :] for c in range(ncol - 2)])

    start = natural(0)
    mask = jnp.where(row < levels, natural(1), 0.0)
    coarse_flow = spread_row(1, levels)
    relaxed = p["relax"] * spread_row(1, levels + 1)
    weight = coarse_weights(mask, coarse_flow, p)
    season = season_of(segment, count, STEPS * 0.5)
    first_coarse = coarse_step(start, mask, weight, coarse_flow, relaxed, season, p)
    end_coarse = cols[2, 0 : ncol - 2]
    rf_out[...] = end_coarse
    rj_out[...] = end_coarse - first_coarse
    stat_out[...] = cols[1, 0 : ncol - 2]
    for t in range(tracers):
        for l in range(levels):
            for h in range(2):
                fine_out[t * levels + l, :, halves[h]] = u[end, t, l + 1, h, 0:own]
    flat = first_coarse.reshape((ncol - 2) * ROWS, LANES)
    for i in range(4):
        fine_out[tracers * levels + i // 2, :, halves[i % 2]] = flat[i * own : (i + 1) * own]


def pack_kernel(rf5, rj4, rj3, rj2, stat, low, high):
    n = rf5.shape[0]
    at = 0
    for ref, width in ((rf5, 4), (rj4, 3), (rj3, 2), (rj2, 1), (stat, 4)):
        low[at : at + width] = ref[0:width]
        high[at : at + width] = ref[n - width : n]
        at += width


def chain_kernel(count, levels, rf5, rj4, rj3, rj2, stat, left, right, rates, out):
    segment = lax.axis_index("tm")
    p = planes_of(rates, levels)
    row = iota((ROWS, LANES), 0)
    own = rf5.shape[0]

    def joined(ref, at, width):
        return jnp.concatenate([left[at : at + width], ref[...], right[at : at + width]])

    coarse = joined(rf5, 0, 4)
    jumps = [joined(rj4, 4, 3), joined(rj3, 7, 2), joined(rj2, 9, 1)]
    mask = jnp.where(row < levels, joined(stat, 10, 4), 0.0)

    def spread_row(r):
        parts = [left[10 + i, pl.ds(r, ROWS, stride=0), :] for i in range(1, 4)]
        parts += [stat[i, pl.ds(r, ROWS, stride=0), :] for i in range(own)]
        parts += [right[10 + i, pl.ds(r, ROWS, stride=0), :] for i in range(0, 3)]
        return jnp.stack(parts)

    flow = spread_row(levels)
    relaxed = p["relax"] * spread_row(levels + 1)
    weight = coarse_weights(mask, flow, p)
    for i in range(SECTIONS):
        back = lax.rem(segment + (count - SECTIONS + i), count)
        season = season_of(back, count, STEPS * 0.5)
        coarse = coarse_step(coarse, mask, weight, flow, relaxed, season, p)
        if i < SECTIONS - 1:
            coarse = coarse + jumps[i]
            mask, weight, flow, relaxed = (v[1:-1] for v in (mask, weight, flow, relaxed))
    out[...] = coarse


def final_kernel(fine, chain, out, wide):
    tracers, levels, own, _ = out.shape
    ncol = chain.shape[0]
    halves = [slice(0, LANES), slice(LANES, 2 * LANES)]
    parts = [fine[tracers * levels + i // 2, :, halves[i % 2]] for i in range(4)]
    begun = jnp.concatenate(parts).reshape(ncol, ROWS, LANES)
    gain = (chain[...] - begun).reshape(ncol * ROWS, LANES)
    for t in range(tracers):
        value = jnp.dot(gain, spread_matrix(t), precision=HIGH, preferred_element_type=F32)
        for h in range(2):
            wide[t, h] = value[:, halves[h]]
    upper = iota((8, LANES), 0) < COARSEN

    def level(l, _):
        for t in range(tracers):
            for i in range(own // 8):
                for h in range(2):
                    a = wide[t, h, pl.ds(2 * i * ROWS + l, 8, stride=0), :]
                    b = wide[t, h, pl.ds((2 * i + 1) * ROWS + l, 8, stride=0), :]
                    rows = slice(8 * i, 8 * i + 8)
                    out[t, l, rows, halves[h]] = (
                        fine[t * levels + l, rows, halves[h]] + jnp.where(upper, a, b)
                    )
        return 0

    lax.fori_loop(0, levels, level, 0)


VM = pl.BlockSpec(memory_space=pltpu.VMEM)
SM = pl.BlockSpec(memory_space=pltpu.SMEM)


def shifted(value, axis, step):
    count = lax.axis_size(axis)
    return lax.ppermute(value, axis, [(i, (i + step) % count) for i in range(count)])


def shards(start_states, wet_levels, advection, forcing, rates):
    state = start_states[0]
    tracers, levels, own, lat = state.shape
    count = lax.axis_size("tm")
    ncol = own // COARSEN
    total = own + 2 * COARSEN
    coarse_shape = jax.ShapeDtypeStruct((ncol, ROWS, LANES), F32)

    def edge(part):
        return jnp.concatenate(
            [
                state[:, :, part].reshape(tracers * levels, COARSEN, lat),
                wet_levels[None, part].astype(F32),
                advection[None, part],
                forcing[None, part],
            ]
        )

    left = shifted(edge(slice(own - COARSEN, own)), "space", 1)
    right = shifted(edge(slice(0, COARSEN)), "space", -1)

    fine, rf, rj, stat = pl.pallas_call(
        functools.partial(fine_kernel, count),
        out_shape=(
            jax.ShapeDtypeStruct((tracers * levels + 2, own, lat), F32),
            coarse_shape, coarse_shape, coarse_shape,
        ),
        in_specs=[VM] * 6 + [SM],
        out_specs=(VM,) * 4,
        scratch_shapes=[
            pltpu.VMEM((2, tracers, levels + 2, 2, total, LANES), F32),
            pltpu.VMEM((levels, 2, total, LANES), F32),
            pltpu.VMEM((levels, 2, total, LANES), F32),
            pltpu.VMEM((5, 2, total, LANES), F32),
            pltpu.VMEM((2, total, LANES), F32),
            pltpu.VMEM((2, total, LANES), F32),
            pltpu.VMEM((tracers, ROWS * ROWS, 2 * LANES), F32),
            pltpu.VMEM((ROWS * ROWS, LANES), F32),
            pltpu.VMEM((3, ncol + 2, ROWS, LANES), F32),
        ],
        cost_estimate=pl.CostEstimate(flops=20_000_000, bytes_accessed=3_000_000, transcendentals=0),
        name="fine",
    )(state, left, right, wet_levels, advection, forcing, rates)

    rf5 = shifted(rf, "tm", 5)
    rj4, rj3, rj2 = (shifted(rj, "tm", j) for j in (4, 3, 2))
    bulk = shifted(fine, "tm", 1)

    halo_shape = jax.ShapeDtypeStruct((14, ROWS, LANES), F32)
    low, high = pl.pallas_call(
        pack_kernel,
        out_shape=(halo_shape, halo_shape),
        in_specs=[VM] * 5,
        out_specs=(VM, VM),
        name="pack",
    )(rf5, rj4, rj3, rj2, stat)
    from_left = shifted(high, "space", 1)
    from_right = shifted(low, "space", -1)
    chain = pl.pallas_call(
        functools.partial(chain_kernel, count, levels),
        out_shape=coarse_shape,
        in_specs=[VM] * 7 + [SM],
        out_specs=VM,
        name="chain",
    )(rf5, rj4, rj3, rj2, stat, from_left, from_right, rates)
    out = pl.pallas_call(
        final_kernel,
        out_shape=jax.ShapeDtypeStruct(state.shape, F32),
        in_specs=[VM, VM],
        out_specs=VM,
        scratch_shapes=[pltpu.VMEM((tracers, 2, ncol * ROWS, LANES), F32)],
        name="final",
    )(bulk, chain)
    return out[None]


def solution(mesh):
    return jax.shard_map(
        shards,
        mesh=mesh,
        in_specs=(
            P("tm", None, None, "space", None),
            P("space", None),
            P("space", None),
            P("space", None),
            P(),
        ),
        out_specs=P("tm", None, None, "space", None),
        check_vma=False,
    )
```
